32 devices in a mesh: dp: 2 (over x), row: 4 (over y, core), col: 4 (over z).
Axes of the slice: x: 2, y: 2, z: 4, core: 2. Of those that a mesh axis runs over, the one named last changes fastest.
Arguments:
- block_input: bfloat16 [4096, 1536], P(('dp', 'row'), 'col'), may hold values from -6 to 6
- teacher: bfloat16 [4096, 1536], P(('dp', 'row'), 'col'), may hold values from -6 to 6
- valid: int32 [8, 512], P(('dp', 'row')), may hold values from 0 to 1, as said below
- segments: int32 [8, 512], P(('dp', 'col')), may hold values from 0 to 3, never falling along the last dimension, each value on 1 to 400 neighbouring positions
- expert_ids: int32 [4096, 8], P('dp'), may hold values from 0 to 39, all different within a row; in each aligned block of 2048 rows (0 to 2047, 2048 to 4095, ...) at most 512 rows name the same one
- gate_probs: float32 [4096, 8], P('dp'), may hold values from 0.05 to 0.25
- norm1_gain: float32 [1536], P('col'), may hold values from 0.5 to 1.5
- w_query: bfloat16 [1536, 1536], P('col', 'row'), may hold values from -0.21875 to 0.21875
- w_key: bfloat16 [1536, 512], P('col', 'row'), may hold values from -0.21875 to 0.21875
- w_value: bfloat16 [1536, 512], P('col', 'row'), may hold values from -0.15625 to 0.15625
- w_out: bfloat16 [1536, 1536], P('row', 'col'), may hold values from -0.625 to 0.625
- norm2_gain: float32 [1536], P('col'), may hold values from 0.5 to 1.5
- w_gate: bfloat16 [40, 1536, 512], P(None, 'col', 'row'), may hold values from -0.15625 to 0.15625
- w_up: bfloat16 [40, 1536, 512], P(None, 'col', 'row'), may hold values from -0.15625 to 0.15625
- w_down: bfloat16 [40, 512, 1536], P(None, 'row', 'col'), may hold values from -0.75 to 0.75
Outputs:
- block_output: bfloat16 [4096, 1536], P(('dp', 'row'), 'col')
- loss: float32 [], replicated
- d_input: float32 [4096, 1536], P(('dp', 'row'), 'col')
- d_norm1: float32 [1536], P('col')
- d_query: float32 [1536, 1536], P(('col', 'dp'), 'row')
- d_key: float32 [1536, 512], P(('col', 'dp'), 'row')
- d_value: float32 [1536, 512], P(('col', 'dp'), 'row')
- d_out: float32 [1536, 1536], P('row', ('col', 'dp'))
- d_norm2: float32 [1536], P('col')
- d_gate: float32 [40, 1536, 512], P(None, ('col', 'dp'), 'row')
- d_up: float32 [40, 1536, 512], P(None, ('col', 'dp'), 'row')
- d_down: float32 [40, 512, 1536], P(None, 'row', ('col', 'dp'))
The draws below stay inside these ranges and needn't reach their ends.
Inputs may be any that keep to these rules, and one draw needn't show every extreme that they name: In each sequence the tokens with valid = 1 come first. `segments`: segment numbers of a sequence never fall and take every value of 0 to 3; a document has 1 to 400 tokens, and some document has exactly 400. `expert_ids`: each token names 8 different experts; among the tokens of one data group no expert is named more than 512 times, and in some group one expert is named exactly 512 times.
All inputs are finite; a program needn't handle non-finite values.
Results may differ from the reference program's by a relative error of at most 0.012.
The reference program's roundings to bfloat16 on the way count: a program that leaves them out, or rounds other values in their place, can miss the bound.
Values may be sent and summed in bfloat16 or wider, within the bound.
No kernel may reach another device: no remote copies, remote signals or barrier semaphores. Data moves between devices by JAX's collectives and lax.ppermute only.
A program may use at most 256 MiB of HBM per device.

```python
import math
import jax
import jax.numpy as jnp
import numpy as np
from jax import lax

D = 1536
H = 24
KV = 8
HD = 64
E = 40
FE = 512
TOPK = 8
SEQ = 512
DOCS = 4
DOC_MOST = 400
TOK_GROUP = 2048
TOKENS = 4096
NSEQ = 8
CAP = 512


def draw_valid(key, part):
    base_length = SEQ // 3
    spread = SEQ - SEQ // 3 - SEQ // 8
    jitter = jax.random.randint(key, (NSEQ,), 0, SEQ // 8 + 1)
    order = jnp.arange(NSEQ, dtype=jnp.int32)
    length = base_length + spread * order // max(NSEQ - 1, 1) + jitter
    place = jnp.arange(SEQ, dtype=jnp.int32)
    return (place[None, :] < length[:, None]).astype(jnp.int32)


def raised(entries, key, source, target, blocks, factor):
    def block_of(position):
        return (jnp.arange(entries.shape[position]) // (entries.shape[position] // blocks)).reshape((-1,) + (1,) * (entries.ndim - 1 - position))

    near = jax.random.permutation(key, blocks)[block_of(target)]
    far = (block_of(target) + blocks // 2) % blocks
    return jnp.where((block_of(source) == near) | (block_of(source) == far), factor * entries, entries)


def levels(own_key, dims, cuts, smallest, largest):
    def one(position, shards_of):
        steps = jax.random.uniform(jax.random.fold_in(jax.random.fold_in(own_key, 6), position), (shards_of,), jnp.float32, smallest / len(cuts), largest / len(cuts))
        return jnp.repeat(jnp.exp(steps), dims[position] // shards_of).reshape((-1,) + (1,) * (len(dims) - position - 1))

    level = one(*cuts[0])
    for cut in cuts[1:]:
        level = level * one(*cut)
    return level


def profile(count, total, bound, skew):
    portions = [(1 << 20) // math.isqrt(grade ** skew) + 1 for grade in range(2, count + 1)]
    rest, given = total - bound - (count - 1), [1] * (count - 1)
    while rest > 0:
        candidates = [i for i in range(count - 1) if given[i] < bound]
        mass, remaining = sum([portions[i] for i in candidates]), rest
        for i in candidates:
            more = min(bound - given[i], max(1, remaining * portions[i] // mass), rest)
            given[i] = given[i] + more
            rest = rest - more
    return np.array([bound] + given)


def ragged_sizes(own_key, count, total, bound, slope):
    if count == 2:
        one = jax.random.randint(own_key, (), max(1, total - bound), min(bound, total - 1) + 1)
        return jnp.stack([one, total - one])
    lengths = jnp.asarray(profile(count, total, bound, slope), jnp.int32)
    twos = (count - 1) // 2
    source_of, sink = lengths[1:1 + 2 * twos:2], lengths[2:2 + 2 * twos:2]
    margin = jnp.minimum(source_of - 1, bound - sink)
    shifted = jax.random.randint(jax.random.fold_in(own_key, 1), (twos,), 0, 1 << 20) % (margin + 1)
    lengths = lengths.at[1:1 + 2 * twos:2].set(source_of - shifted).at[2:2 + 2 * twos:2].set(sink + shifted)
    return lengths[jax.random.permutation(jax.random.fold_in(own_key, 2), count)]


def routed_block(own_key, own, number, rows, number_of, top, limit, skew):
    sequence = jax.random.permutation(own_key, number_of)
    heavy_load, usual = shares(number_of, rows * top, limit, skew, True), shares(number_of, rows * top, limit, skew, False)
    places = jnp.arange(number_of)

    def named(tallies, offset_by):
        used = int((tallies > 0).sum())
        fixed = max(1, used // 4)
        shifted = fixed + (places - fixed + offset_by * (used - fixed)) % max(1, number_of - fixed)
        return jnp.zeros((number_of,), jnp.int32).at[sequence[jnp.where(places < fixed, places, shifted)]].set(jnp.asarray(tallies, jnp.int32))

    tallies = jnp.where(number % 4 == 0, named(heavy_load, number // 4), named(usual, number - number // 4 - 1))
    mixed = jax.random.permutation(jax.random.fold_in(own, 3), number_of)
    donor, receiver = mixed[0:number_of // 2 * 2:2], mixed[1:number_of // 2 * 2:2]
    margin = jnp.minimum(tallies[donor] - 1, limit - tallies[receiver]) // 2
    margin = jnp.where((donor == sequence[0]) | (receiver == sequence[0]) | (tallies[receiver] == 0), 0, jnp.maximum(margin, 0))
    shifted = jax.random.randint(jax.random.fold_in(own, 4), (number_of // 2,), 0, 1 << 20) % (margin + 1)
    tallies = tallies.at[donor].add(-shifted).at[receiver].add(shifted)
    items = jnp.searchsorted(jnp.cumsum(tallies), jnp.arange(rows * top), side="right").astype(jnp.int32)
    table = items.reshape(top, rows).T
    table = table[jax.random.permutation(jax.random.fold_in(own, 1), rows)]
    offset_by = jax.random.randint(jax.random.fold_in(own, 2), (rows, 1), 0, top)
    return jnp.take_along_axis(table, (jnp.arange(top)[None, :] + offset_by) % top, axis=1)


def shares(amount, total, reach, slope, full):
    portions = [(1 << 20) // math.isqrt(rank ** slope) + 1 for rank in range(1, amount + 1)]
    largest = reach if full else min(reach, max(-(-total // amount), total * portions[0] // sum(portions)))
    least = 1 if total - largest >= amount - 1 else 0
    given, rest = [largest] + [least] * (amount - 1), total - largest - least * (amount - 1)
    while rest > 0:
        candidates = [i for i in range(1, amount) if given[i] < largest] or [i for i in range(1, amount) if given[i] < reach]
        mass, left = sum([portions[i] for i in candidates]), rest
        for i in candidates:
            addition = min(reach - given[i], max(1, left * portions[i] // mass), rest)
            given[i] = given[i] + addition
            rest = rest - addition
    return np.array(given)


def normal_values(key, shape, deviation, limit, split=(), kind=jnp.bfloat16):
    drawn = jax.random.normal(key, shape, jnp.float32) * deviation
    if len(split) > 0:
        drawn = levels(key, shape, split, -0.22, 0.18) * drawn
    return jnp.clip(drawn, min=-limit, max=limit).astype(kind)


def noise_with(own_key, extent, scale, reach, cuts, heavy, held_as=jnp.bfloat16):
    entries = scale * jax.random.normal(own_key, extent, jnp.float32)
    if cuts:
        entries = entries * levels(own_key, extent, cuts, -0.22, 0.18)
    return jnp.clip(raised(entries, jax.random.fold_in(own_key, 3), *heavy), -reach, reach).astype(held_as)


def setup_inputs(seed: int = 0) -> dict:
    splits = jax.random.split(jax.random.key(seed), 16)
    block_input = normal_values(splits[0], (TOKENS, D), 1.0, 6.0, ((0, 8), (1, 4)))
    teacher = noise_with(splits[1], (TOKENS, D), 1.0, 6.0, ((0, 8), (1, 4)), (0, 1, 8, 2.0))
    valid = draw_valid(jax.random.fold_in(splits[15], 71), 0)
    segments = jax.vmap(lambda own: jnp.searchsorted(jnp.cumsum(ragged_sizes(own, DOCS, SEQ, DOC_MOST, 1)), jnp.arange(SEQ), side="right"))(jax.random.split(splits[3], NSEQ)).reshape((NSEQ, SEQ)).astype(jnp.int32)
    expert_ids_keys = jax.random.split(jax.random.fold_in(splits[4], 1), TOKENS // TOK_GROUP)
    expert_ids_turns = jax.random.permutation(jax.random.fold_in(splits[4], 3), TOKENS // TOK_GROUP)
    expert_ids = jax.vmap(lambda own, number: routed_block(jax.random.fold_in(splits[4], 2), own, number, TOK_GROUP, E, TOPK, CAP, 1))(expert_ids_keys, expert_ids_turns).reshape((TOKENS, TOPK))
    gate_probs = jnp.clip(0.05 + 0.2 * jax.random.uniform(splits[5], (TOKENS, TOPK), jnp.float32) ** levels(splits[5], (TOKENS, TOPK), ((0, 2),), -0.2, 0.2), 0.05, 0.25)
    norm1_gain = jnp.clip(1.0 + 0.1 * jax.random.normal(splits[6], (D,), jnp.float32), 0.5, 1.5)
    w_query = normal_values(splits[7], (D, H * HD), (D // 2) ** -0.5, 0.21875, ((0, 4), (1, 4)))
    w_key = normal_values(splits[8], (D, KV * HD), (D // 2) ** -0.5, 0.21875, ((0, 4), (1, 4)))
    w_value = normal_values(splits[9], (D, KV * HD), D ** -0.5, 0.15625, ((0, 4), (1, 4)))
    w_out = normal_values(splits[10], (H * HD, D), (H * HD // 16) ** -0.5, 0.625, ((0, 4), (1, 4)))
    norm2_gain = jnp.clip(1.0 + 0.1 * jax.random.normal(splits[11], (D,), jnp.float32), 0.5, 1.5)
    w_gate = normal_values(splits[12], (E, D, FE), D ** -0.5, 0.15625, ((1, 4), (2, 4)))
    w_up = normal_values(splits[13], (E, D, FE), D ** -0.5, 0.15625, ((1, 4), (2, 4)))
    w_down = normal_values(splits[14], (E, FE, D), (FE // 8) ** -0.5, 0.75, ((1, 4), (2, 4)))
    return dict(block_input=block_input, teacher=teacher, valid=valid, segments=segments, expert_ids=expert_ids, gate_probs=gate_probs, norm1_gain=norm1_gain, w_query=w_query, w_key=w_key, w_value=w_value, w_out=w_out, norm2_gain=norm2_gain, w_gate=w_gate, w_up=w_up, w_down=w_down)


@jax.custom_vjp
def low(v):
    return lax.optimization_barrier(v.astype(jnp.bfloat16)).astype(jnp.float32)

@jax.custom_vjp
def low_back(v):
    return v

def low_keep(v):
    return (low(v), None)

def low_pass(kept, grad):
    return (grad,)

def back_keep(v):
    return (v, None)

def back_low(kept, grad):
    return (low(grad),)
low.defvjp(low_keep, low_pass)
low_back.defvjp(back_keep, back_low)
EPS = 1e-06
THETA = 10000.0
NEG = -1e+30
HIGH = lax.Precision.HIGHEST

def rope_tables(length, width):
    half = width // 2
    freq = THETA ** (-(jnp.arange(half, dtype=jnp.float32) * 2.0 / width))
    angle = jnp.arange(length, dtype=jnp.float32)[:, None] * freq[None, :]
    return (jnp.cos(angle), jnp.sin(angle))

def rotate(value, cosine, sine):
    half = value.shape[-1] // 2
    first = value[..., :half]
    second = value[..., half:]
    cosine_wide = cosine[:, None, :]
    sine_wide = sine[:, None, :]
    return jnp.concatenate([first * cosine_wide - second * sine_wide, second * cosine_wide + first * sine_wide], axis=-1)

def rms_norm(value, gain):
    factor = lax.rsqrt(lax.optimization_barrier(jnp.mean(value * value, axis=-1, keepdims=True)) + EPS)
    return low(value * factor * gain)

def attend(queries, keys, values, segment):
    length = queries.shape[0]
    grouped = queries.reshape(length, KV, H // KV, HD)
    scores = jnp.einsum('qkgd,skd->kgqs', grouped, keys, precision=HIGH) * HD ** (-0.5)
    scores = low_back(scores)
    place = jnp.arange(length, dtype=jnp.int32)
    allowed = (segment[:, None] == segment[None, :]) & (place[None, :] <= place[:, None])
    scores = jnp.where(allowed, scores, NEG)
    weights = jax.nn.softmax(scores, axis=-1)
    mixed = jnp.einsum('kgqs,skd->qkgd', low(weights), values, precision=HIGH)
    return low(low_back(mixed.reshape(length, H * HD)))

def experts_layer(normed, route, gate, w_gate, w_up, w_down):
    rows = normed.shape[0]
    width = normed.shape[1]
    onehot = (route[:, :, None] == jnp.arange(E, dtype=jnp.int32)[None, None, :]).astype(jnp.int32)
    counts = lax.optimization_barrier(jnp.sum(onehot, axis=1))
    before = jnp.cumsum(counts, axis=0) - counts
    slot = lax.optimization_barrier(jnp.sum(before[:, None, :] * onehot, axis=2))
    owner = jnp.broadcast_to(jnp.arange(rows, dtype=jnp.int32)[:, None], route.shape)
    table = jnp.full((CAP, E), rows, jnp.int32).at[slot, route].set(owner)
    weight = jnp.zeros((CAP, E), jnp.float32).at[slot, route].set(gate)
    padded = jnp.concatenate([normed, jnp.zeros((1, width), jnp.float32)], axis=0)
    routed = padded[table]
    gate_pre = low_back(jnp.einsum('ced,edf->cef', routed, w_gate, precision=HIGH))
    up_pre = low_back(jnp.einsum('ced,edf->cef', routed, w_up, precision=HIGH))
    inner = low(weight[:, :, None] * jax.nn.silu(gate_pre) * up_pre)
    partial_out = jnp.einsum('cef,efd->ced', inner, w_down, precision=HIGH)
    summed = jnp.zeros((rows + 1, width), jnp.float32).at[table.reshape(-1)].add(partial_out.reshape(-1, width))
    return low_back(summed[:rows])

def group_layer(params, states, target, mask, segment, route, gate, factor):
    gain1, w_query, w_key, w_value, w_out, gain2, w_gate, w_up, w_down = params
    normed1 = rms_norm(states, gain1)
    proj_q = low_back(jnp.dot(normed1, w_query, precision=HIGH))
    proj_k = low_back(jnp.dot(normed1, w_key, precision=HIGH))
    proj_v = low_back(jnp.dot(normed1, w_value, precision=HIGH))
    count_seq = states.shape[0] // SEQ
    cosine, sine = rope_tables(SEQ, HD)
    queries = low(rotate(proj_q.reshape(count_seq, SEQ, H, HD), cosine, sine))
    keys = low(rotate(proj_k.reshape(count_seq, SEQ, KV, HD), cosine, sine))
    values = low(proj_v.reshape(count_seq, SEQ, KV, HD))
    mixed = lax.map(lambda parts: attend(parts[0], parts[1], parts[2], parts[3]), (queries, keys, values, segment))
    attn = low_back(jnp.dot(mixed.reshape(-1, H * HD), w_out, precision=HIGH))
    resid = states + attn
    normed2 = rms_norm(resid, gain2)
    output_state = resid + experts_layer(normed2, route, gate, w_gate, w_up, w_down)
    diff = output_state - target
    return (output_state, factor * jnp.sum(mask[:, None] * diff * diff))

def reference(block_input, teacher, valid, segments, expert_ids, gate_probs, norm1_gain, w_query, w_key, w_value, w_out, norm2_gain, w_gate, w_up, w_down):
    groups = block_input.shape[0] // TOK_GROUP
    inputs = block_input.astype(jnp.float32).reshape(groups, TOK_GROUP, D)
    targets = teacher.astype(jnp.float32).reshape(groups, TOK_GROUP, D)
    masks = valid.astype(jnp.float32).reshape(groups, TOK_GROUP)
    segs_all = segments.reshape(groups, TOK_GROUP // SEQ, SEQ)
    routes = expert_ids.reshape(groups, TOK_GROUP, TOPK)
    gates = gate_probs.reshape(groups, TOK_GROUP, TOPK)
    counted = jnp.sum(masks)
    factor = TOKENS / (2.0 * counted)
    params = tuple((array_in.astype(jnp.float32) for array_in in (norm1_gain, w_query, w_key, w_value, w_out, norm2_gain, w_gate, w_up, w_down)))
    step = jax.checkpoint(group_layer)

    def forward(weights, states_all):

        def advance(running, pieces):
            state, target, mask, segment, route, gate = pieces
            out_state, part = step(weights, state, target, mask, segment, route, gate, factor)
            return (running + part, out_state)
        running, outputs = lax.scan(advance, jnp.zeros((), jnp.float32), (states_all, targets, masks, segs_all, routes, gates))
        return (outputs, running)
    (outputs, running), pullback = jax.vjp(forward, params, inputs)
    d_params, d_inputs = pullback((jnp.zeros_like(outputs), jnp.ones((), jnp.float32)))
    loss = running * 2.0 / (TOKENS * D)
    block_output = outputs.reshape(TOKENS, D).astype(jnp.bfloat16)
    return (block_output, loss, d_inputs.reshape(TOKENS, D), d_params[0], d_params[1], d_params[2], d_params[3], d_params[4], d_params[5], d_params[6], d_params[7], d_params[8])
```

```python
import jax
import jax.numpy as jnp
from jax import lax
from jax.sharding import PartitionSpec as P

HD = 64
SEQ = 512
EPS = 1e-06
THETA = 10000.0
NEG = -1e30

F32 = jnp.float32
BF16 = jnp.bfloat16


def rope_tables(length, width):
    half = width // 2
    freq = THETA ** (-(jnp.arange(half, dtype=F32) * 2.0 / width))
    angle = jnp.arange(length, dtype=F32)[:, None] * freq[None, :]
    return (jnp.cos(angle), jnp.sin(angle))


def rotate(value, cosine, sine):
    first, second = jnp.split(value, 2, axis=-1)
    cosine, sine = cosine[:, None, :], sine[:, None, :]
    return jnp.concatenate(
        [first * cosine - second * sine, second * cosine + first * sine], axis=-1
    )


def rotate_back(incoming, cosine, sine):
    return rotate(incoming, cosine, -sine)


def dot(a, b):
    return jnp.dot(a, b, preferred_element_type=F32)


def dot_t(a, b):
    return lax.dot_general(a, b, (((1,), (1,)), ((), ())), preferred_element_type=F32)


def t_dot(a, b):
    return lax.dot_general(a, b, (((0,), (0,)), ((), ())), preferred_element_type=F32)


def swap(value, axis, bit):
    size = lax.axis_size(axis)
    return lax.ppermute(value, axis, [(i, i ^ bit) for i in range(size)])


def total(value, axes):
    for axis in axes:
        bit = 1
        while bit < lax.axis_size(axis):
            value = value + swap(value, axis, bit)
            bit *= 2
    return value


def transposed(value):
    rows, cols = lax.axis_size("row"), lax.axis_size("col")
    perm = [(i * cols + j, j * rows + i) for i in range(rows) for j in range(cols)]
    return lax.ppermute(value, ("row", "col"), perm)


def all_to_all_cols(pieces, axis):
    cols, col = lax.axis_size("col"), lax.axis_index("col")
    shape = list(pieces.shape[1:])
    step = shape[axis]
    shape[axis] = step * cols
    result = jnp.zeros(shape, pieces.dtype)
    for bit in range(cols):
        peer = col ^ bit
        part = lax.dynamic_index_in_dim(pieces, peer, 0, keepdims=False)
        if bit:
            part = swap(part, "col", bit)
        result = lax.dynamic_update_slice_in_dim(result, part, peer * step, axis)
    return result


def attention_scores(queries, keys, segment):
    length = segment.shape[0]
    scores = jnp.einsum("kgqd,ksd->kgqs", queries, keys, preferred_element_type=F32)
    place = jnp.arange(length, dtype=jnp.int32)
    allowed = (segment[:, None] == segment[None, :]) & (place[None, :] <= place[:, None])
    return jnp.where(allowed, scores * HD ** (-0.5), NEG)


def attend_forward(queries, keys, values, segment):
    scores = attention_scores(queries, keys, segment)
    highest = jnp.max(scores, axis=-1, keepdims=True)
    expo = jnp.exp(scores - highest)
    summed = jnp.sum(expo, axis=-1, keepdims=True)
    probs = (expo / summed).astype(BF16)
    mixed = jnp.einsum("kgqs,ksd->kgqd", probs, values, preferred_element_type=F32)
    return (mixed.astype(BF16), highest + jnp.log(summed))


def attend_backward(queries, keys, values, segment, logsum, d_mixed):
    scores = attention_scores(queries, keys, segment)
    probs = jnp.exp(scores - logsum)
    d_probs = jnp.einsum("kgqd,ksd->kgqs", d_mixed, values, preferred_element_type=F32)
    delta = jnp.sum(probs * d_probs, axis=-1, keepdims=True)
    d_scores = (probs * (d_probs - delta)).astype(BF16)
    scale = HD ** (-0.5)
    d_queries = jnp.einsum("kgqs,ksd->kgqd", d_scores, keys, preferred_element_type=F32) * scale
    d_keys = jnp.einsum("kgqs,kgqd->ksd", d_scores, queries, preferred_element_type=F32) * scale
    d_values = jnp.einsum(
        "kgqs,kgqd->ksd", probs.astype(BF16), d_mixed, preferred_element_type=F32
    )
    return (d_queries, d_keys, d_values)


def local(
    block_input,
    teacher,
    valid,
    segments,
    expert_ids,
    gate_probs,
    norm1_gain,
    w_query,
    w_key,
    w_value,
    w_out,
    norm2_gain,
    w_gate,
    w_up,
    w_down,
):
    tok_row, width_col = block_input.shape
    cols, col = lax.axis_size("col"), lax.axis_index("col")
    rows = lax.axis_size("row")
    groups, group = lax.axis_size("dp"), lax.axis_index("dp")
    width = width_col * cols
    tok_dev = tok_row // cols
    tok_group = tok_row * rows
    count_seq = tok_row // SEQ
    q_width = w_query.shape[1]
    k_width = w_key.shape[1]
    qkv_width = q_width + 2 * k_width
    kv_heads = k_width // HD
    per_kv = q_width // k_width
    experts = w_gate.shape[0]
    hidden = w_gate.shape[2]
    own_experts = experts // cols
    half_experts = own_experts // 2
    parity = group % 2

    states = lax.all_gather(block_input, "col", axis=1, tiled=True)
    packed = jnp.concatenate([w_query, w_key, w_value, w_out], axis=1)
    gathered = lax.all_gather(transposed(packed), "row", axis=0, tiled=True)
    w_qkv = gathered[:, :qkv_width]
    w_o = gathered[:, qkv_width:].reshape(rows, q_width, width_col)
    segment = transposed(segments)
    gains = all_to_all_cols(
        jnp.broadcast_to(jnp.stack([norm1_gain, norm2_gain])[None], (cols, 2, width_col)), 1
    )
    gain1, gain2 = gains[0], gains[1]
    mask_row = valid.reshape(-1).astype(F32)
    count = total(jnp.broadcast_to(jnp.sum(mask_row), (8, 128)), ("dp", "row"))[0, 0]
    teacher_own = all_to_all_cols(
        teacher.reshape(cols, tok_dev, width_col), 1
    )

    def fetch(weight, axis, turn):
        picked = weight.reshape(cols, 2, half_experts, weight.shape[1], weight.shape[2])
        picked = lax.dynamic_index_in_dim(picked, parity, 1, keepdims=False)
        if turn:
            picked = picked.transpose(0, 2, 1, 3)
            picked = picked.reshape(cols, weight.shape[1], half_experts * hidden)
        else:
            picked = picked.reshape(cols, half_experts * hidden, weight.shape[2])
        own = all_to_all_cols(picked, axis)
        return own, swap(own, "dp", 1)

    gate_a, gate_b = fetch(w_gate, 0, True)
    up_a, up_b = fetch(w_up, 0, True)
    down_a, down_b = fetch(w_down, 1, False)

    states32 = states.astype(F32)
    scale1 = lax.rsqrt(jnp.mean(states32 * states32, axis=1) + EPS)
    normed1 = (states32 * scale1[:, None] * gain1).astype(BF16)
    projected = dot(normed1, w_qkv)
    cosine, sine = rope_tables(SEQ, HD)

    def q_heads(value):
        return value.reshape(SEQ, kv_heads, per_kv, HD).transpose(1, 2, 0, 3)

    def q_flat(value):
        return value.transpose(2, 0, 1, 3).reshape(SEQ, q_width)

    def k_heads(value):
        return value.reshape(SEQ, kv_heads, HD).transpose(1, 0, 2)

    def k_flat(value):
        return value.transpose(1, 0, 2).reshape(SEQ, k_width)

    def turned(value, turn):
        return turn(value.reshape(SEQ, -1, HD), cosine, sine).reshape(SEQ, -1)

    kept, mixed = [], []
    for number in range(count_seq):
        part = projected[number * SEQ : (number + 1) * SEQ]
        queries = q_heads(turned(part[:, :q_width], rotate).astype(BF16))
        keys = k_heads(turned(part[:, q_width : q_width + k_width], rotate).astype(BF16))
        values = k_heads(part[:, q_width + k_width :].astype(BF16))
        out, logsum = attend_forward(queries, keys, values, segment[number])
        kept.append((queries, keys, values, segment[number], logsum))
        mixed.append(q_flat(out))
    mixed = jnp.concatenate(mixed, axis=0)
    attn_part = jnp.einsum("th,rhd->trd", mixed, w_o, preferred_element_type=F32)
    attn_part = attn_part.reshape(tok_row, width).astype(BF16)
    attn = lax.psum_scatter(attn_part, "col", scatter_dimension=0, tiled=True)
    states_own = lax.dynamic_slice_in_dim(states, col * tok_dev, tok_dev, 0)
    resid = states_own.astype(F32) + attn.astype(F32)
    scale2 = lax.rsqrt(jnp.mean(resid * resid, axis=1) + EPS)
    normed2 = (resid * scale2[:, None] * gain2).astype(BF16)

    tokens = lax.all_gather(normed2, ("row", "col"), axis=0, tiled=True)
    base = col * own_experts

    def gates_of(half):
        names = base + half * half_experts + jnp.arange(half_experts, dtype=jnp.int32)
        hit = expert_ids[:, :, None] == names[None, None, :]
        return jnp.sum(jnp.where(hit, gate_probs[:, :, None], 0.0), axis=1)

    halves = ((gate_a, up_a, down_a, parity), (gate_b, up_b, down_b, 1 - parity))
    saved = []
    expert_part = None
    for w_g, w_u, w_d, half in halves:
        gates = jnp.repeat(gates_of(half), hidden, axis=1)
        gate_pre = dot(tokens, w_g)
        up_pre = dot(tokens, w_u)
        inner = (gates * gate_pre * jax.nn.sigmoid(gate_pre) * up_pre).astype(BF16)
        part = dot(inner, w_d)
        expert_part = part if expert_part is None else expert_part + part
        saved.append((gates, gate_pre, up_pre, inner))
    expert_sum = lax.psum_scatter(
        expert_part.astype(BF16), ("row", "col"), scatter_dimension=0, tiled=True
    )
    output = resid + expert_sum.astype(F32)

    mask = lax.dynamic_slice_in_dim(mask_row, col * tok_dev, tok_dev, 0)[:, None]
    diff = output - teacher_own.astype(F32)
    squared = jnp.sum(mask * diff * diff)
    grad_out = mask * diff * (tok_group * groups / count)
    grads = lax.all_gather(grad_out.astype(BF16), ("row", "col"), axis=0, tiled=True)

    def own_columns(value):
        return all_to_all_cols(
            value.reshape(tok_dev, cols, width_col).transpose(1, 0, 2), 0
        )

    block_output = own_columns(output.astype(BF16))

    d_tokens = None
    d_gates, d_ups, d_downs = [], [], []
    for (w_g, w_u, w_d, half), (gates, gate_pre, up_pre, inner) in zip(halves, saved):
        scaled = gates * dot_t(grads, w_d)
        sigma = jax.nn.sigmoid(gate_pre)
        d_up_pre = (scaled * gate_pre * sigma).astype(BF16)
        d_gate_pre = (scaled * up_pre * sigma * (1.0 + gate_pre * (1.0 - sigma))).astype(BF16)
        part = dot_t(d_gate_pre, w_g) + dot_t(d_up_pre, w_u)
        d_tokens = part if d_tokens is None else d_tokens + part
        d_downs.append(t_dot(inner, grads))
        d_gates.append(t_dot(tokens, d_gate_pre))
        d_ups.append(t_dot(tokens, d_up_pre))
    d_normed2 = lax.psum_scatter(
        d_tokens.astype(BF16), ("row", "col"), scatter_dimension=0, tiled=True
    ).astype(F32)

    def over_groups(value, axis):
        if groups == 2:
            keep = lax.dynamic_index_in_dim(value, group, axis, keepdims=False)
            send = lax.dynamic_index_in_dim(value, 1 - group, axis, keepdims=False)
            return keep + swap(send.astype(BF16), "dp", 1).astype(F32)
        moved = jnp.moveaxis(value, axis, 0).astype(BF16)
        return lax.psum_scatter(moved, "dp", scatter_dimension=0, tiled=False).astype(F32)

    def in_order(pair):
        first = jnp.where(parity == 0, pair[0], pair[1])
        second = jnp.where(parity == 0, pair[1], pair[0])
        return first, second

    part_width = width_col // groups

    def give_turned(pair):
        result = []
        for value in in_order(pair):
            value = over_groups(value.reshape(cols, groups, part_width, -1), 1).astype(BF16)
            moved = all_to_all_cols(value[:, None], 0)
            moved = moved.reshape(cols, part_width, half_experts, hidden).astype(F32)
            result.append(moved.transpose(0, 2, 1, 3))
        return jnp.stack(result, axis=1).reshape(experts, part_width, hidden)

    def give_down(pair):
        result = []
        for value in in_order(pair):
            value = over_groups(value.reshape(-1, cols, groups, part_width), 2).astype(BF16)
            moved = all_to_all_cols(value.transpose(1, 0, 2)[:, None], 0)
            result.append(moved.reshape(cols, half_experts, hidden, part_width).astype(F32))
        return jnp.stack(result, axis=1).reshape(experts, hidden, part_width)

    d_down = give_down(d_downs)
    d_gate = give_turned(d_gates)
    d_up = give_turned(d_ups)

    dotted = jnp.sum(d_normed2 * gain2 * resid, axis=1, keepdims=True)
    d_resid = (
        grad_out
        + scale2[:, None] * gain2 * d_normed2
        - resid * (scale2[:, None] ** 3 * dotted / width)
    )
    d_gain2_part = jnp.sum(d_normed2 * resid * scale2[:, None], axis=0)
    sums = jnp.concatenate([d_gain2_part, jnp.broadcast_to(squared, (512,))]).reshape(-1, 128)
    sums = total(sums, ("dp", "row", "col")).reshape(-1)
    d_gain2 = lax.dynamic_slice_in_dim(sums, col * width_col, width_col, 0)
    loss = sums[width] / (width * count)
    g_attn = lax.all_gather(d_resid.astype(BF16), "col", axis=0, tiled=True)
    d_resid_cols = own_columns(d_resid)
    d_mixed = jnp.einsum(
        "trd,rhd->th", g_attn.reshape(tok_row, rows, width_col), w_o, preferred_element_type=F32
    ).astype(BF16)
    d_out = jnp.einsum(
        "th,trd->rhd", mixed, g_attn.reshape(tok_row, rows, width_col), preferred_element_type=F32
    )
    d_proj = []
    for number in range(count_seq):
        part = d_mixed[number * SEQ : (number + 1) * SEQ]
        d_queries, d_keys, d_values = attend_backward(*kept[number], q_heads(part))
        d_proj.append(
            jnp.concatenate(
                [
                    turned(q_flat(d_queries), rotate_back),
                    turned(k_flat(d_keys), rotate_back),
                    k_flat(d_values),
                ],
                axis=1,
            ).astype(BF16)
        )
    d_proj = jnp.concatenate(d_proj, axis=0)
    d_normed1_part = dot_t(d_proj, w_qkv)
    d_normed1 = lax.psum_scatter(
        d_normed1_part.astype(BF16), "col", scatter_dimension=1, tiled=True
    ).astype(F32)
    dotted1 = total(
        jnp.sum(d_normed1_part * gain1 * states32, axis=1).reshape(-1, 128), ("col",)
    ).reshape(tok_row, 1)
    states_col = block_input.astype(F32)
    d_input = (
        d_resid_cols
        + scale1[:, None] * norm1_gain * d_normed1
        - states_col * (scale1[:, None] ** 3 * dotted1 / width)
    )
    d_gain1 = total(
        jnp.sum(d_normed1 * states_col * scale1[:, None], axis=0).reshape(-1, 128), ("dp", "row")
    ).reshape(-1)

    def over_rows(value):
        return lax.psum_scatter(
            value.astype(BF16), "row", scatter_dimension=0, tiled=False
        ).astype(F32)

    d_qkv = over_rows(t_dot(normed1, d_proj).reshape(rows, width_col, qkv_width))
    d_qkv = over_groups(d_qkv.reshape(groups, part_width, qkv_width), 0)
    d_qkv = transposed(d_qkv.astype(BF16)).astype(F32)
    d_out = over_rows(d_out)
    d_out = over_groups(d_out.reshape(q_width, groups, part_width), 1)
    d_out = transposed(d_out.astype(BF16)).astype(F32)
    return (
        block_output,
        loss,
        d_input,
        d_gain1,
        d_qkv[:, :q_width],
        d_qkv[:, q_width : q_width + k_width],
        d_qkv[:, q_width + k_width :],
        d_out,
        d_gain2,
        d_gate,
        d_up,
        d_down,
    )


def solution(mesh):
    placed = (
        P(("dp", "row"), "col"),
        P(("dp", "row"), "col"),
        P(("dp", "row"), None),
        P(("dp", "col"), None),
        P("dp", None),
        P("dp", None),
        P("col"),
        P("col", "row"),
        P("col", "row"),
        P("col", "row"),
        P("row", "col"),
        P("col"),
        P(None, "col", "row"),
        P(None, "col", "row"),
        P(None, "row", "col"),
    )
    return jax.shard_map(
        local,
        mesh=mesh,
        in_specs=placed,
        out_specs=(
            P(("dp", "row"), "col"),
            P(),
            P(("dp", "row"), "col"),
            P("col"),
            P(("col", "dp"), "row"),
            P(("col", "dp"), "row"),
            P(("col", "dp"), "row"),
            P("row", ("col", "dp")),
            P("col"),
            P(None, ("col", "dp"), "row"),
            P(None, ("col", "dp"), "row"),
            P(None, "row", ("col", "dp")),
        ),
        check_vma=False,
    )
```
